256 devices in a mesh: samples: 16 (over x, z_hi), genes: 8 (over z_lo, y), tissues: 2 (over core).
Axes of the slice: x: 4, y: 4, z: 8 (z_hi: 4, z_lo: 2; z = z_hi * 2 + z_lo), core: 2. Of those that a mesh axis runs over, the one named last changes fastest.
Arguments:
- dosage: bfloat16 [256, 8192, 128], P('genes', 'samples')
- traits: bfloat16 [8192, 256], P('samples'), may hold values from -6 to 6
- weights: bfloat16 [512, 48, 512], P('genes', 'tissues'), may hold values from -0.25 to 0.25
- block_mask: int32 [512, 48, 4], P('genes', 'tissues'), may hold values 0 or 1
- window_start: int32 [512], replicated, may hold values from 0 to 252, as said below
- precision_matrix: float32 [48, 48], replicated, as said below
Outputs:
- combined: float32 [512, 256], P('genes', 'samples')
- heterogeneity: float32 [512, 256], P('genes', 'samples')
The draws below stay inside these ranges and needn't reach their ends.
Inputs may be any that keep to these rules, and one draw needn't show every extreme that they name: Gene g's cis window is the 4 consecutive blocks from window_start[g], all held by one device along genes (blocks b * 32 to (b + 1) * 32 - 1 on index b). Of the genes of one device along genes, at most 16 have their windows on one holder, and exactly 16 on some holder. `precision_matrix`: Symmetric, each diagonal entry larger than the sum of magnitudes off the diagonal in its row.
All inputs are finite; a program needn't handle non-finite values. No bound on the sum of `block_mask` on one device may be relied on, other than what follows from the above.
Results may differ from the reference program's by a relative error of at most 0.0029.
Values may be sent and summed in bfloat16 or wider, within the bound.
A program may use at most 192 MiB of HBM per device.

```python
import jax
import jax.numpy as jnp
from jax import lax

G_DEV = 64
NB_DEV = 32
BLOCK = 128
WIN = 4
TISSUES = 48
TRAITS = 256
GCAP = 16
GENES = 512
BLOCKS = 256
SAMPLES = 8192
N_GENES = 8


def draw_dosage(key, part):
    key_base = jax.random.fold_in(key, 11)
    key_cols = jax.random.fold_in(key, 12)
    rising = 0.6 * 3.0 ** (jnp.arange(SAMPLES, dtype=jnp.float32) / max(SAMPLES - 1, 1))
    base = jax.random.normal(key_base, (BLOCKS, SAMPLES, BLOCK), jnp.float32)
    base = jnp.clip(base, -5.0, 5.0)
    rows = rising
    cols = jnp.exp(jax.random.uniform(key_cols, (BLOCKS, 1, BLOCK), jnp.float32, -0.7, 0.7))
    return (base * rows[None, :, None] * cols).astype(jnp.bfloat16)


def owner_windows(key, owner):
    key_main = jax.random.fold_in(key, 1)
    key_rest = jax.random.fold_in(key, 2)
    key_order = jax.random.fold_in(key, 3)
    key_offset = jax.random.fold_in(key, 4)
    drawn_holder = jax.random.randint(key_main, (), 0, N_GENES)
    main_holder = jnp.where(owner == N_GENES - 1, N_GENES - 1, jnp.where(owner == 0, 0, drawn_holder)).astype(jnp.int32)
    index_list = jnp.arange((N_GENES - 1) * GCAP, dtype=jnp.int32) // GCAP
    others = index_list + (index_list >= main_holder).astype(jnp.int32)
    shuffled = jax.random.permutation(key_rest, others)
    holders = jnp.concatenate([jnp.full((GCAP,), main_holder, jnp.int32), shuffled[:G_DEV - GCAP]])
    offsets = jax.random.randint(key_offset, (G_DEV,), 0, NB_DEV - WIN + 1).astype(jnp.int32)
    offsets = offsets.at[0].set(NB_DEV - WIN).at[1].set(0)
    order = jax.random.permutation(key_order, G_DEV)
    return (holders[order] * NB_DEV + offsets[order]).astype(jnp.int32)


def draw_window_start(key, part):
    owners = jnp.arange(N_GENES, dtype=jnp.int32)
    owner_keys = jax.vmap(lambda index: jax.random.fold_in(key, 100 + index))(owners)
    starts = jax.vmap(owner_windows)(owner_keys, owners)
    return starts.reshape(GENES)


def draw_precision_matrix(key, part):
    key_off = jax.random.fold_in(key, 21)
    key_diag = jax.random.fold_in(key, 22)
    raw = jax.random.uniform(key_off, (TISSUES, TISSUES), jnp.float32, -1.0, 1.0) / TISSUES
    symmetric = (raw + raw.T) * 0.5
    eye_mask = jnp.eye(TISSUES, dtype=jnp.float32)
    diag = jax.random.uniform(key_diag, (TISSUES,), jnp.float32, 1.0, 2.0)
    return symmetric * (1.0 - eye_mask) + eye_mask * diag[None, :]


def plant(drawn, rng, low, largest):
    shape = drawn.shape
    spot = [jax.random.randint(jax.random.fold_in(rng, axis), (), 0, shape[axis]) for axis in range(len(shape))]
    drawn = drawn.at[tuple(spot)].set(low)
    longest = shape.index(max(shape))
    spot[longest] = (spot[longest] + 1) % shape[longest]
    return drawn.at[tuple(spot)].set(largest)


def levels(rng, dims, cuts, smallest, high):
    loudness = 1.0
    for position, shards_of in cuts:
        heights = jax.random.uniform(jax.random.fold_in(jax.random.fold_in(rng, 6), position), (shards_of,), jnp.float32, smallest / len(cuts), high / len(cuts))
        loudness = loudness * jnp.repeat(jnp.exp(heights), dims[position] // shards_of).reshape((-1,) + (1,) * (len(dims) - 1 - position))
    return loudness


def noise(rng, dims, scale, limit, pieces=(), kind=jnp.bfloat16):
    entries = jax.random.normal(rng, dims, jnp.float32) * scale
    if len(pieces) > 0:
        entries = levels(rng, dims, pieces, -0.22, 0.18) * entries
    return jnp.clip(entries, min=-limit, max=limit).astype(kind)


def setup_inputs(seed: int = 0) -> dict:
    key_list = jax.random.split(jax.random.key(seed), 7)
    return {
        "dosage": draw_dosage(jax.random.fold_in(key_list[6], 71), 0),
        "traits": noise(key_list[1], (SAMPLES, TRAITS), 1.0, 6.0, ((0, 16),)),
        "weights": noise(key_list[2], (GENES, TISSUES, WIN * BLOCK), (WIN * BLOCK) ** -0.5, 0.25, ((0, 8), (1, 2))),
        "block_mask": plant((jax.random.randint(key_list[3], (GENES, TISSUES, WIN), 0, 4) < 3).astype(jnp.int32), jax.random.fold_in(key_list[3], 1), 0, 1),
        "window_start": draw_window_start(jax.random.fold_in(key_list[6], 71), 0),
        "precision_matrix": draw_precision_matrix(jax.random.fold_in(key_list[6], 71), 0),
    }


def reference(dosage, traits, weights, block_mask, window_start, precision_matrix):
    shaped = weights.reshape(GENES, TISSUES, WIN, BLOCK)
    masked = shaped * block_mask[..., None].astype(jnp.bfloat16)

    def one_gene(pair):
        start, gene_weights = pair
        window = lax.dynamic_slice_in_dim(dosage, start.astype(jnp.int32), WIN, 0)
        total = jnp.einsum('wsv,twv->ts', window.astype(jnp.float32), gene_weights.astype(jnp.float32))
        return total.astype(jnp.bfloat16)
    predicted = lax.map(one_gene, (window_start, masked))
    pred_wide = predicted.astype(jnp.float32)
    products = jnp.einsum('gts,sk->gtk', pred_wide, traits.astype(jnp.float32))
    squares = lax.optimization_barrier(jnp.sum(pred_wide * pred_wide, axis=2))
    scores = products / jnp.sqrt(squares[..., None] + 1.0)
    row_sums = lax.optimization_barrier(jnp.sum(precision_matrix, axis=1))
    grand_total = jnp.sum(row_sums)
    weighted = jnp.einsum('tu,guk->gtk', precision_matrix, scores, precision=lax.Precision.HIGHEST)
    linear = jnp.einsum('t,gtk->gk', row_sums, scores, precision=lax.Precision.HIGHEST)
    quadratic = lax.optimization_barrier(jnp.sum(scores * weighted, axis=1))
    combined = linear / jnp.sqrt(grand_total)
    heterogeneity = (quadratic - linear * linear / grand_total) / TISSUES
    return (combined, heterogeneity)
```

```python
import jax
import jax.numpy as jnp
from jax import lax
from jax.experimental import pallas as pl
from jax.experimental.pallas import tpu as pltpu
from jax.sharding import PartitionSpec as P

TISSUES = 48
MESH = pl.DeviceIdType.MESH
F32 = jnp.float32
BF16 = jnp.bfloat16
RING = 4
WIN = 4
PAIR = 2 * WIN
PARTS = 2
HALVES = 2


def halve(value):
    high = value.astype(BF16)
    return high, (value - high.astype(F32)).astype(BF16)


def merge(target, sources):
    cross = [ref[:WIN].astype(F32) + ref[WIN:PAIR].astype(F32) for ref in sources]
    high, low = halve(sum(cross[1:], cross[0]))
    target[:WIN] = high
    target[WIN:PAIR] = low
    gram = [ref[PAIR:].astype(F32) for ref in sources]
    target[PAIR:] = sum(gram[1:], gram[0]).astype(BF16)


def merge_all(target, sources):
    if len(target.shape) == 3:
        merge(target, sources)
        return

    def step(i, carry):
        merge(target.at[i], [ref.at[i] for ref in sources])
        return carry

    lax.fori_loop(0, target.shape[0], step, 0)


def kernel(
    start_ref, dosage_ref, traits_ref, masked_ref, precision_ref, out_ref,
    flipped, traits_t, send, xin, ysum, zin, table, mine, squares, partial, received, prods, result,
    send_sem, recv_sem, local_sem,
):
    samples, genes, core = lax.axis_index("samples"), lax.axis_index("genes"), lax.axis_index("tissues")
    x, zh = samples // RING, samples % RING
    zl, y = genes // RING, genes % RING
    block_count = dosage_ref.shape[0]
    half_blocks = block_count // 2
    groups = half_blocks // WIN
    per_part = half_blocks // PARTS
    gene_half = mine.shape[0]
    kmine = table.shape[2]
    base = core * half_blocks

    def turn(value, by):
        return (value + by + RING) % RING

    def at_x(to):
        return {"samples": to * RING + zh, "genes": genes, "tissues": core}

    def at_z(to):
        return {"samples": x * RING + to, "genes": genes, "tissues": core}

    def at_y(to):
        return {"samples": samples, "genes": zl * RING + to, "tissues": core}

    twin = {"samples": samples, "genes": (1 - zl) * RING + y, "tissues": core}
    partner = {"samples": samples, "genes": genes, "tissues": 1 - core}

    barrier = pltpu.get_barrier_semaphore()
    peers = [at_x(turn(x, k)) for k in (1, 2, 3)] + [at_z(turn(zh, k)) for k in (1, 2, 3)]
    peers += [at_y(turn(y, 1)), at_y(turn(y, -1)), twin, partner]
    for peer in peers:
        pl.semaphore_signal(barrier, inc=1, device_id=peer, device_id_type=MESH)

    counter = [0]
    started = []

    def copy(src, dst, to):
        index = counter[0]
        counter[0] += 1
        made = pltpu.make_async_remote_copy(
            src_ref=src, dst_ref=dst, send_sem=send_sem.at[index], recv_sem=recv_sem.at[index],
            device_id=to, device_id_type=MESH,
        )
        made.start()
        started.append(made)
        return index

    def arrival(index, dst):
        pltpu.make_async_remote_copy(
            src_ref=dst, dst_ref=dst, send_sem=send_sem.at[index], recv_sem=recv_sem.at[index],
            device_id=partner, device_id_type=MESH,
        ).wait_recv()

    own_copy = pltpu.make_async_copy(
        masked_ref.at[pl.ds(core * gene_half, gene_half)], mine.at[:, :, core], local_sem.at[0]
    )
    own_copy.start()

    traits_t[...] = traits_ref[...].T

    def flip(i, carry):
        flipped[i] = dosage_ref[jnp.maximum(base + i - (WIN - 1), 0)].T
        return carry

    lax.fori_loop(0, half_blocks + WIN - 1, flip, 0)

    def compute(part):
        def step(i, carry):
            local = part * per_part + i
            group, j = local // WIN, local % WIN
            block = dosage_ref[base + local]
            high, low = halve(jnp.dot(traits_t[...], block, preferred_element_type=F32))
            high = high.reshape(RING, RING, kmine, block.shape[1])
            low = low.reshape(RING, RING, kmine, block.shape[1])
            for ix in range(RING):
                send[ix, group, :, j] = high[ix]
                send[ix, group, :, j + WIN] = low[ix]
            left = flipped[pl.ds(local, WIN)]
            left = left.reshape(WIN * left.shape[1], left.shape[2])
            gram = jnp.dot(left, block, preferred_element_type=F32).astype(BF16)
            gram = gram.reshape(WIN, block.shape[1] // kmine, kmine, block.shape[1])
            for d in range(WIN):
                send[j, group, d, PAIR:] = gram[WIN - 1 - d]
            return carry

        lax.fori_loop(0, per_part, step, 0)

    class Scatter:
        def __init__(self, part, chunk, landing, at, me):
            self.part, self.chunk, self.landing, self.at, self.me = part, chunk, landing, at, me
            self.right, self.left, self.far = turn(me, 1), turn(me, -1), turn(me, 2)

        def spot(self, half, kind):
            return self.landing.at[self.part, half, kind]

        def group(self, half):
            return self.part * HALVES + half

        def send_far(self):
            self.far0 = copy(self.chunk(self.far, self.group(0)), self.spot(0, 0), self.at(self.right))
            self.far1 = copy(self.chunk(self.far, self.group(1)), self.spot(1, 0), self.at(self.left))

        def send_near(self):
            self.near0 = copy(self.chunk(self.left, self.group(0)), self.spot(0, 2), self.at(self.left))
            self.near1 = copy(self.chunk(self.right, self.group(1)), self.spot(1, 2), self.at(self.right))

        def relay(self):
            for half, index, to in ((0, self.far0, self.right), (1, self.far1, self.left)):
                spot = self.spot(half, 0)
                arrival(index, spot)
                merge_all(spot, [spot, self.chunk(to, self.group(half))])
                index = copy(spot, self.spot(half, 1), self.at(to))
                if half == 0:
                    self.sum0 = index
                else:
                    self.sum1 = index

        def total(self, half, target):
            arrival((self.near0, self.near1)[half], self.spot(half, 2))
            arrival((self.sum0, self.sum1)[half], self.spot(half, 1))
            merge_all(target, [self.chunk(self.me, self.group(half)), self.spot(half, 1), self.spot(half, 2)])

    xs = [Scatter(p, lambda to, group: send.at[to, group], xin, at_x, x) for p in range(PARTS)]
    zs = [Scatter(p, lambda to, group: ysum.at[group, to], zin, at_z, zh) for p in range(PARTS)]

    def slot(gene_index, part):
        return (gene_index * 2 + core) * groups + part * HALVES

    def other_slot(gene_index, part):
        return (gene_index * 2 + 1 - core) * groups + part * HALVES

    arrivals = []

    def to_partner(gene_index, part, half=None):
        first = slot(gene_index, part) + (half or 0)
        size = HALVES if half is None else 1
        ref = table.at[pl.ds(first, size)]
        index = copy(ref, ref, partner)
        arrivals.append((index, table.at[pl.ds(other_slot(gene_index, part) + (half or 0), size)]))

    class Gather:
        def __init__(self, part):
            self.part = part

        def chunk(self, gene_index, half=None):
            if half is None:
                return table.at[pl.ds(slot(gene_index, self.part), HALVES)]
            return table.at[pl.ds(slot(gene_index, self.part) + half, 1)]

        def send_y(self, gene_index):
            ref = self.chunk(gene_index)
            return copy(ref, ref, at_y(turn(y, 1))), copy(ref, ref, at_y(turn(y, -1)))

        def begin(self):
            for half in range(HALVES):
                zs[self.part].total(half, table.at[slot(genes, self.part) + half])
            own = self.chunk(genes)
            self.twin = copy(own, own, twin)
            self.first = self.send_y(genes)
            to_partner(genes, self.part)

        def middle(self):
            other = (1 - zl) * RING + y
            arrival(self.twin, self.chunk(other))
            self.second = self.send_y(other)
            to_partner(other, self.part)

        def forward(self, zone, indices):
            fromleft, fromright = zone * RING + turn(y, -1), zone * RING + turn(y, 1)
            arrival(indices[0], self.chunk(fromleft))
            ref = self.chunk(fromleft, 0)
            onward0 = copy(ref, ref, at_y(turn(y, 1)))
            to_partner(fromleft, self.part)
            arrival(indices[1], self.chunk(fromright))
            ref = self.chunk(fromright, 1)
            onward1 = copy(ref, ref, at_y(turn(y, -1)))
            to_partner(fromright, self.part)
            return onward0, onward1

        def finish(self, zone, onward):
            far = zone * RING + turn(y, 2)
            for half in range(HALVES):
                arrival(onward[half], self.chunk(far, half))
                to_partner(far, self.part, half)

        def spread(self):
            self.onward0 = self.forward(zl, self.first)
            self.onward1 = self.forward(1 - zl, self.second)

        def end(self):
            self.finish(zl, self.onward0)
            self.finish(1 - zl, self.onward1)

    gs = [Gather(p) for p in range(PARTS)]

    def x_total(part):
        for half in range(HALVES):
            xs[part].total(half, ysum.at[part * HALVES + half])
        zs[part].send_far()
        zs[part].send_near()

    compute(0)
    pl.semaphore_wait(barrier, len(peers))
    xs[0].send_far()
    xs[0].send_near()
    half_sent = copy(masked_ref.at[pl.ds((1 - core) * gene_half, gene_half)], mine.at[:, :, core], partner)
    compute(1)
    xs[1].send_far()
    xs[0].relay()
    xs[1].send_near()
    xs[1].relay()
    x_total(0)
    zs[0].relay()
    x_total(1)
    gs[0].begin()
    zs[1].relay()
    gs[0].middle()
    gs[0].spread()
    gs[1].begin()
    gs[1].middle()
    gs[0].end()
    gs[1].spread()
    gs[1].end()
    own_copy.wait()
    arrival(half_sent, mine.at[:, :, 1 - core])
    for index, ref in arrivals:
        arrival(index, ref)

    rows = mine.shape[2] * mine.shape[3]
    width = mine.shape[4]
    lanes = lax.broadcasted_iota(jnp.int32, (rows, width), 1)
    first_gene = (genes * 2 + core) * gene_half
    twice = jnp.where(zh == 0, 1.0, 2.0).astype(F32)
    squares[...] = jnp.zeros_like(squares)

    def square_step(g, carry):
        start = start_ref[first_gene + g]
        offset = (x + WIN - start % WIN) % WIN
        back = jnp.maximum(offset - zh, 0)
        scale = jnp.where(offset >= zh, twice, 0.0)
        pair = table[(start + offset) // WIN, PAIR:].reshape(width, width)
        near = mine[g, back].reshape(rows, width)
        far = mine[g, offset].reshape(rows, width)
        applied = jnp.dot(near, pair, preferred_element_type=F32) * far.astype(F32)
        total = jnp.sum(applied, axis=1, keepdims=True) * scale
        squares[...] += jnp.where(lanes == g, total, 0.0)
        return carry

    lax.fori_loop(0, gene_half, square_step, 0, unroll=8)

    def swap(stage, source, at, me):
        return [copy(source, received.at[stage, k - 1], at(turn(me, k))) for k in (1, 2, 3)]

    x_swap = swap(0, squares, at_x, x)

    def product_group(group, carry):
        for j in range(8):
            g = group * 8 + j
            start = start_ref[first_gene + g]
            spots = [((start + w) // WIN, (start + w) % WIN) for w in range(WIN)]
            tiles = [table[at, tile] for at, tile in spots]
            tiles += [table[at, tile + WIN] for at, tile in spots]
            rights = jnp.concatenate(tiles, axis=1)
            lefts = jnp.concatenate([mine[g, w].reshape(rows, width) for w in range(WIN)] * 2, axis=1)
            prods[group, :, j * kmine:(j + 1) * kmine] = lax.dot_general(
                lefts, rights, (((1,), (1,)), ((), ())), preferred_element_type=F32
            )
        return carry

    chunk_groups = gene_half // 8
    lax.fori_loop(0, chunk_groups // 2, product_group, 0)
    for k, index in enumerate(x_swap):
        arrival(index, received.at[0, k])
    partial[...] = squares[...] + received[0, 0] + received[0, 1] + received[0, 2]
    z_swap = swap(1, partial, at_z, zh)
    lax.fori_loop(chunk_groups // 2, chunk_groups, product_group, 0)
    for k, index in enumerate(z_swap):
        arrival(index, received.at[1, k])
    total = partial[...] + received[1, 0] + received[1, 1] + received[1, 2]

    columns = gene_half * kmine
    root = jnp.sqrt(jnp.maximum(total, 0.0) + 1.0)
    spread_rows = lax.broadcasted_iota(jnp.int32, (width, columns), 0)
    spread_cols = lax.broadcasted_iota(jnp.int32, (width, columns), 1)
    spread = (spread_rows == spread_cols // kmine).astype(F32)
    roots = jnp.dot(root, spread, preferred_element_type=F32, precision=lax.Precision.HIGHEST)
    products = jnp.concatenate([prods[i] for i in range(chunk_groups)], axis=1)
    scores = products / roots
    matrix = precision_ref[...]
    row_sums = jnp.sum(matrix, axis=1, keepdims=True)
    grand_total = jnp.sum(row_sums, axis=0, keepdims=True)
    weighted = jnp.dot(matrix, scores, preferred_element_type=F32, precision=lax.Precision.HIGHEST)
    linear = jnp.sum(row_sums * scores, axis=0, keepdims=True)
    quadratic = jnp.sum(scores * weighted, axis=0, keepdims=True)
    combined = linear / jnp.sqrt(grand_total)
    heterogeneity = (quadratic - linear * linear / grand_total) / TISSUES
    row = lax.broadcasted_iota(jnp.int32, (8, columns), 0)
    result[core] = jnp.where(row == 0, combined, heterogeneity)
    last = copy(result.at[core], result.at[core], partner)
    arrival(last, result.at[1 - core])
    out_ref[...] = result[...]
    for made in started:
        made.wait_send()


def on_device(dosage, traits, weights, block_mask, window_start, precision_matrix):
    block_count, sample_rows, block_len = dosage.shape
    gene_rows, tissue_cols, _ = weights.shape
    window_len = block_mask.shape[2]
    padded = (tissue_cols + 15) // 16 * 16
    ring_count = lax.axis_size("samples")
    trait_cols = traits.shape[1] // ring_count
    owners = lax.axis_size("genes")
    gene_half = gene_rows // 2
    shaped = weights.reshape(gene_rows, tissue_cols, window_len, block_len)
    masked = shaped * block_mask[..., None].astype(BF16)
    masked = jnp.transpose(masked, (0, 2, 1, 3))
    masked = jnp.pad(masked, ((0, 0), (0, 0), (0, padded - tissue_cols), (0, 0)))
    matrix = precision_matrix.reshape(2, tissue_cols, 2, tissue_cols)
    pad = (0, padded - tissue_cols)
    matrix = jnp.pad(matrix, ((0, 0), pad, (0, 0), pad)).reshape(2 * padded, 2 * padded)

    half_blocks = block_count // 2
    groups = half_blocks // WIN
    tiles = PAIR + block_len // trait_cols
    unit = (tiles, trait_cols, block_len)
    rows = 2 * padded
    columns = gene_half * trait_cols
    vmem = pl.BlockSpec(memory_space=pltpu.VMEM)
    copies = PARTS * (6 + 6 + 9 + 10) + 8
    out = pl.pallas_call(
        kernel,
        out_shape=jax.ShapeDtypeStruct((2, 8, columns), F32),
        in_specs=[pl.BlockSpec(memory_space=pltpu.SMEM), vmem, vmem, vmem, vmem],
        out_specs=vmem,
        scratch_shapes=[
            pltpu.VMEM((half_blocks + WIN - 1, block_len, sample_rows), BF16),
            pltpu.VMEM((traits.shape[1], sample_rows), BF16),
            pltpu.VMEM((RING, groups, RING) + unit, BF16),
            pltpu.VMEM((PARTS, HALVES, 3, RING) + unit, BF16),
            pltpu.VMEM((groups, RING) + unit, BF16),
            pltpu.VMEM((PARTS, HALVES, 3) + unit, BF16),
            pltpu.VMEM((owners * 2 * groups,) + unit, BF16),
            pltpu.VMEM((gene_half, window_len, 2, padded, block_len), BF16),
            pltpu.VMEM((rows, block_len), F32),
            pltpu.VMEM((rows, block_len), F32),
            pltpu.VMEM((2, 3, rows, block_len), F32),
            pltpu.VMEM((gene_half // 8, rows, 8 * trait_cols), F32),
            pltpu.VMEM((2, 8, columns), F32),
            pltpu.SemaphoreType.DMA((copies,)),
            pltpu.SemaphoreType.DMA((copies,)),
            pltpu.SemaphoreType.DMA((1,)),
        ],
        compiler_params=pltpu.CompilerParams(
            collective_id=0, has_side_effects=True, vmem_limit_bytes=60 * 1024 * 1024
        ),
        name="twas",
    )(window_start, dosage, traits, masked, matrix)
    combined = out[:, 0, :].reshape(gene_rows, trait_cols)
    heterogeneity = out[:, 1, :].reshape(gene_rows, trait_cols)
    return (combined, heterogeneity)


def solution(mesh):
    in_specs = (
        P("genes", "samples", None),
        P("samples", None),
        P("genes", "tissues", None),
        P("genes", "tissues", None),
        P(),
        P(),
    )
    out_specs = (P("genes", "samples"), P("genes", "samples"))
    return jax.shard_map(
        on_device, mesh=mesh, in_specs=in_specs, out_specs=out_specs, check_vma=False
    )
```
